32 devices in a mesh: row: 16 (over z, y, core), col: 2 (over x).
Axes of the slice: x: 2, y: 2, z: 4, core: 2. Of those that a mesh axis runs over, the one named last changes fastest.
Arguments:
- residues: int32 [512], P('row'), may hold values from 0 to 20
- embed_table: bfloat16 [21, 256], replicated, may hold values from -6 to 6
- conv_first: bfloat16 [4352, 256], replicated, may hold values from -0.09375 to 0.09375
- conv_second: bfloat16 [4352, 256], replicated, may hold values from -0.09375 to 0.09375
- proj_row: bfloat16 [256, 64], replicated, may hold values from -0.375 to 0.375
- proj_col: bfloat16 [256, 64], replicated, may hold values from -0.375 to 0.375
- pair_weights: bfloat16 [4, 64, 576], replicated, may hold values from -0.25 to 0.25
Outputs:
- pair_out: bfloat16 [64, 512, 512], P(None, 'row', 'col')
The draws below stay inside these ranges and needn't reach their ends.
All inputs are finite; a program needn't handle non-finite values.
Results may differ from the reference program's by a relative error of at most 0.018.
Values may be sent and summed in bfloat16 or wider, within the bound.
A program may use at most 64 MiB of HBM per device.

```python
import jax
import jax.numpy as jnp
from jax import lax

W = 256
C = 64
VOCAB = 21
KERNEL = 17
LAYERS = 4
WINDOW = 512


def place_ends(entries, key, smallest, high):
    index_at = [jax.random.randint(jax.random.fold_in(key, axis), (), 0, length) for axis, length in enumerate(entries.shape)]
    main_axis = entries.shape.index(max(entries.shape))
    neighbour = index_at[:main_axis] + [(index_at[main_axis] + 1) % entries.shape[main_axis]] + index_at[main_axis + 1:]
    return entries.at[tuple(index_at)].set(smallest).at[tuple(neighbour)].set(high)


def scatter_about(stream_key, dims, scale, reach, kind=jnp.bfloat16):
    entries = jax.random.normal(stream_key, dims, jnp.float32) * scale
    return jnp.minimum(jnp.maximum(entries, -reach), reach).astype(kind)


def setup_inputs(seed: int = 0) -> dict:
    key_of = jax.random.split(jax.random.key(seed), 8)
    return {
        "residues": place_ends(jax.random.randint(key_of[0], (WINDOW,), 0, VOCAB), jax.random.fold_in(key_of[0], 1), 0, VOCAB - 1).astype(jnp.int32),
        "embed_table": scatter_about(key_of[1], (VOCAB, W), 1.0, 6.0),
        "conv_first": scatter_about(key_of[2], (KERNEL * W, W), (KERNEL * W) ** -0.5, 0.09375),
        "conv_second": scatter_about(key_of[3], (KERNEL * W, W), (KERNEL * W) ** -0.5, 0.09375),
        "proj_row": scatter_about(key_of[4], (W, C), W ** -0.5, 0.375),
        "proj_col": scatter_about(key_of[5], (W, C), W ** -0.5, 0.375),
        "pair_weights": scatter_about(key_of[6], (LAYERS, C, 9 * C), (9 * C) ** -0.5, 0.25),
    }


def elu(v):
    return jnp.where(v > 0, v, jnp.expm1(jnp.minimum(v, 0.0)))


def conv_seq(feats, weight_stack):
    half = KERNEL // 2
    length = feats.shape[0]
    padded = jnp.pad(feats, ((half, half), (0, 0)))
    windows = jnp.concatenate([padded[k:k + length] for k in range(KERNEL)], axis=1)
    return jnp.dot(windows, weight_stack, preferred_element_type=jnp.float32)


def reference(residues, embed_table, conv_first, conv_second, proj_row, proj_col, pair_weights):
    onehot = (residues[:, None] == jnp.arange(VOCAB, dtype=jnp.int32)[None, :]).astype(jnp.bfloat16)
    embedded = jnp.dot(onehot, embed_table, preferred_element_type=jnp.float32).astype(jnp.bfloat16)
    first = elu(conv_seq(embedded, conv_first)).astype(jnp.bfloat16)
    second = (first.astype(jnp.float32) + elu(conv_seq(first, conv_second))).astype(jnp.bfloat16)
    left = jnp.dot(second, proj_row, preferred_element_type=jnp.float32).astype(jnp.bfloat16)
    right = jnp.dot(second, proj_col, preferred_element_type=jnp.float32).astype(jnp.bfloat16)
    pair_features = (left.T.astype(jnp.float32)[:, :, None] + right.T.astype(jnp.float32)[:, None, :]).astype(jnp.bfloat16)
    for layer_number in range(LAYERS):
        dilation_rate = 2 ** layer_number
        activation_map = elu(pair_features.astype(jnp.float32)).astype(jnp.bfloat16).astype(jnp.float32)
        filter_kernel = pair_weights[layer_number].astype(jnp.float32).reshape(C, 3, 3, C).transpose(0, 3, 1, 2)
        output_map = lax.conv_general_dilated(activation_map[None], filter_kernel, (1, 1), ((dilation_rate, dilation_rate), (dilation_rate, dilation_rate)), rhs_dilation=(dilation_rate, dilation_rate), dimension_numbers=("NCHW", "OIHW", "NCHW"), precision=lax.Precision.HIGHEST)[0]
        pair_features = (pair_features.astype(jnp.float32) + output_map).astype(jnp.bfloat16)
    return pair_features
```

```python
import functools

import jax
import jax.numpy as jnp
from jax import lax
from jax.experimental import pallas as pl
from jax.experimental.pallas import tpu as pltpu
from jax.sharding import PartitionSpec as P

MESH = pl.DeviceIdType.MESH
PAD = 8
STRIPS = 16
CHUNKS = 4
HALO = 16
F32, BF16 = jnp.float32, jnp.bfloat16


def elu(v):
    return jnp.maximum(v, jnp.exp(jnp.minimum(v, 0.0)) - 1.0)


def sequence_kernel(
    dims, res_hbm, table_hbm, w1_hbm, w2_hbm, prow_hbm, pcol_hbm, pw_hbm, left_out, right_out, bw,
    res_ref, table_ref, w1_ref, w2_ref, prow_ref, pcol_ref, pw_ref, sems, send_sem, recv_sem, tab, emb, xs, fs, cols, la, lb, right_ref,
):
    rows, ncol, span, tile, chans, kernel, layers = dims
    me_r, me_c = lax.axis_index("row"), lax.axis_index("col")
    window = rows * span
    width = table_ref.shape[1]
    half = kernel // 2
    edge = 2 * HALO
    n_row, n_col = span + 2 * edge, tile + 2 * edge
    height, wide = span + 2 * HALO, tile + 2 * HALO
    two = 2 * chans

    barrier = pltpu.get_barrier_semaphore()
    for k in range(1, rows):
        pl.semaphore_signal(
            barrier, inc=1, device_id={"row": lax.rem(me_r + k, rows)}, device_id_type=MESH
        )
    pairs = (
        (pw_hbm, pw_ref), (res_hbm, res_ref.at[me_r]), (table_hbm, table_ref), (w1_hbm, w1_ref),
        (w2_hbm, w2_ref), (prow_hbm, prow_ref), (pcol_hbm, pcol_ref),
    )
    loads = [pltpu.make_async_copy(a, b, sems.at[i]) for i, (a, b) in enumerate(pairs)]
    for load in loads:
        load.start()
    loads[0].wait()

    zero = jnp.zeros((chans, chans), BF16)
    for layer in range(layers):
        w = pw_ref[layer].astype(F32).T.astype(BF16)
        for g, offset in enumerate((0, 1, 2, -1)):
            line = []
            for tx in range(3):
                for h in range(2):
                    ty = offset - h + 1
                    tap = 3 * ty + tx
                    here = 0 <= ty <= 2
                    line.append(w[tap * chans : (tap + 1) * chans] if here else zero)
            bw[layer, g * chans : (g + 1) * chans, :] = jnp.concatenate(line, axis=1)
    n_pair = height // 2

    pl.semaphore_wait(barrier, rows - 1)
    copies = [
        pltpu.make_async_remote_copy(
            src_ref=res_hbm,
            dst_ref=res_ref.at[me_r],
            send_sem=send_sem.at[k],
            recv_sem=recv_sem.at[k],
            device_id={"row": lax.rem(me_r + k, rows)},
            device_id_type=MESH,
        )
        for k in range(1, rows)
    ]
    for copy in copies:
        copy.start()

    loads[2].wait()
    tab[...] = jnp.zeros_like(tab)
    tab[0 : table_ref.shape[0], :] = table_ref[...]
    emb[0:edge, :] = jnp.zeros((edge, width), F32)
    emb[edge + window : 2 * edge + window, :] = jnp.zeros((edge, width), F32)
    loads[1].wait()
    for copy in copies:
        copy.wait()
    per = 128 // span
    vocab = lax.broadcasted_iota(jnp.int32, (tab.shape[0], 128), 0)
    for g in range(window // 128):
        line = jnp.concatenate([res_ref[per * g + m] for m in range(per)], axis=1)
        hot = (jnp.broadcast_to(line, vocab.shape) == vocab).astype(F32).astype(BF16)
        emb[edge + 128 * g : edge + 128 * (g + 1), :] = lax.dot_general(
            hot, tab[...], (((0,), (0,)), ((), ())), preferred_element_type=F32
        )
    xs[0:n_row, :] = emb[pl.ds(pl.multiple_of(me_r * span, span), n_row), :]
    xs[n_row : n_row + n_col, :] = emb[pl.ds(pl.multiple_of(me_c * tile, tile), n_col), :]

    n_first = n_row + n_col - 2 * half
    n_second = n_first - 2 * half
    for k in range(kernel):
        cols[:, k * width : (k + 1) * width] = xs[k : k + n_first, :].astype(BF16)
    loads[3].wait()
    first = elu(jnp.dot(cols[...], w1_ref[...], preferred_element_type=F32))
    at = lax.broadcasted_iota(jnp.int32, (n_first, width), 0) + half
    pos = at + jnp.where(at < n_row, me_r * span - edge, me_c * tile - edge - n_row)
    first = jnp.where((pos >= 0) & (pos < window), first, 0.0)
    fs[...] = first.astype(BF16).astype(F32)
    for k in range(kernel):
        cols[0:n_second, k * width : (k + 1) * width] = fs[k : k + n_second, :].astype(BF16)
    loads[4].wait()
    second = elu(jnp.dot(cols[0:n_second, :], w2_ref[...], preferred_element_type=F32))
    second = (fs[half : half + n_second, :] + second).astype(BF16)

    loads[5].wait()
    loads[6].wait()
    blank = jnp.zeros((chans, width), BF16)
    pr, pc = prow_ref[...], pcol_ref[...]
    s_row, s_col = second[0:height], second[n_row : n_row + wide]
    dot = functools.partial(jnp.dot, preferred_element_type=F32)

    def project(x, *parts):
        w = jnp.concatenate(parts, axis=0)
        y = lax.dot_general(x, w, (((1,), (1,)), ((), ())), preferred_element_type=F32)
        return y.astype(BF16).astype(F32)

    la[...] = project(s_row, pr, blank)
    lb[...] = project(s_row, blank, pr)
    right_ref[...] = project(s_col, pc, pc)
    left_out[...] = la[pl.ds(0, n_pair, stride=2), :] + lb[pl.ds(1, n_pair, stride=2), :]
    slabs = wide // STRIPS
    for m in range(slabs):
        right_out[STRIPS * m : STRIPS * (m + 1)] = right_ref[pl.ds(m, STRIPS, stride=slabs), :]


def pair_kernel(
    dims, left_ref, right_ref, bw_hbm, out_hbm, bw, pair, act_a, act_b, lin, stage, outv, masks, sems
):
    rows, ncol, span, tile, chans, layers = dims
    me_r, me_c = lax.axis_index("row"), lax.axis_index("col")
    n_pair = (span + 2 * HALO) // 2
    wide, two = tile + 2 * HALO, 2 * chans
    slabs = wide // STRIPS
    load = pltpu.make_async_copy(bw_hbm, bw, sems.at[0])
    load.start()

    at = lax.broadcasted_iota(jnp.int32, (wide, two), 0)
    col = lax.rem(at, STRIPS) * slabs + lax.div(at, STRIPS)
    inside = ((col >= HALO) | (me_c > 0)) & ((col < HALO + tile) | (me_c < ncol - 1))
    inside = jnp.where(inside, 1.0, 0.0)
    masks[0] = inside.astype(BF16)
    masks[1] = (inside * (me_r > 0).astype(F32)).astype(BF16)
    masks[2] = (inside * (me_r < rows - 1).astype(F32)).astype(BF16)
    blank = jnp.zeros((PAD, wide, two), BF16)
    for act in (act_a, act_b):
        act[0:PAD] = blank
        act[PAD + n_pair : 2 * PAD + n_pair] = blank
    lane = lax.broadcasted_iota(jnp.int32, (wide, two), 1)
    low_bf16 = lane.astype(F32).astype(BF16) < jnp.asarray(chans, BF16)
    low_half = lane < chans

    def put(act, p, value):
        pair[p] = value
        which = 1 if p < HALO // 2 else 2 if p >= n_pair - HALO // 2 else 0
        act[p + PAD] = elu(value).astype(BF16) * masks[which]

    def start(p):
        put(act_a, p, right_ref[...] + left_ref[p : p + 1, :])

    def add(p, m, part):
        at = pl.ds(STRIPS * m, STRIPS)
        pair[p, at, :] = pair[p, at, :] + part

    def conv(layer, src, d, slots):
        lhs = jnp.concatenate(
            [
                jnp.concatenate(
                    [src[p + PAD], jnp.where(low_bf16, src[p + PAD + d], src[p + PAD - d])], axis=1
                )
                for p in slots
            ],
            axis=0,
        )
        got = jnp.dot(lhs, bw[layer], preferred_element_type=F32)
        for k, p in enumerate(slots):
            for m in range(slabs):
                row = got[k * wide + STRIPS * m : k * wide + STRIPS * (m + 1)]
                to = m + d
                part = row[:, 0:two]
                add(p, to % slabs, part if to < slabs else pltpu.roll(part, 1, 0))
                add(p, m, row[:, two : 2 * two])
                to = m - d
                part = row[:, 2 * two : 3 * two]
                add(p, to % slabs, part if to >= 0 else pltpu.roll(part, STRIPS - 1, 0))
        return [pair[p] for p in slots]

    bufs = (act_a, act_b)
    for layer in range(layers - 1):
        src, dst = bufs[layer % 2], bufs[(layer + 1) % 2]
        d = 2**layer
        units = [(q + d, n_pair - 2 * d + q) for q in range(d)]
        n_rim = len(units)
        units += [
            (2 * d * (q // d) + q % d, 2 * d * (q // d) + q % d + d)
            for q in range(d, n_pair // 2 - d)
        ]
        if layer == 0:
            for p in range(n_pair):
                start(p)
            load.wait()
        for u, slots in enumerate(units):
            one, other = conv(layer, src, d, slots)
            if u < n_rim:
                new = [pltpu.roll(one, chans, 1), one, other, pltpu.roll(other, chans, 1)]
                slots = [u, u + d, n_pair - 2 * d + u, n_pair - d + u]
            else:
                new = [
                    jnp.where(low_half, one, pltpu.roll(other, chans, 1)),
                    jnp.where(low_half, pltpu.roll(one, chans, 1), other),
                ]
            for p, value in zip(slots, new):
                put(dst, p, value)

    src = bufs[(layers - 1) % 2]
    d = 2 ** (layers - 1)
    halves = tile // 128
    for u in range((n_pair - HALO) // 2):
        slots = (HALO // 2 + 2 * u, HALO // 2 + 2 * u + 1)
        for k, value in enumerate(conv(layers - 1, src, d, slots)):
            b = lin.at[(2 * u + k) % 4]
            for m in range(slabs):
                b[pl.ds(m, STRIPS, stride=slabs), :] = value[STRIPS * m : STRIPS * (m + 1)]
            turned = b[HALO : HALO + tile, :].T
            at = slots[k] - HALO // 2
            line = 2 * d * (at // d) + at % d
            for h in range(halves):
                block = turned[:, 128 * h : 128 * (h + 1)]
                stage[h, pl.ds(line, chans, stride=span), :] = block[0:chans]
                stage[h, pl.ds(line + d, chans, stride=span), :] = block[chans:two]
    step = chans // CHUNKS
    saves = []
    for g in range(CHUNKS):
        for c in range(g * step, (g + 1) * step):
            for h in range(halves):
                outv[c, :, 128 * h : 128 * (h + 1)] = stage[h, c * span : (c + 1) * span, :].astype(BF16)
        part = pl.ds(g * step, step)
        saves.append(pltpu.make_async_copy(outv.at[part], out_hbm.at[part], sems.at[1 + g]))
        saves[-1].start()
    for save in saves:
        save.wait()


def local(residues, embed_table, conv_first, conv_second, proj_row, proj_col, pair_weights):
    rows, ncol = lax.axis_size("row"), lax.axis_size("col")
    span = residues.shape[0]
    window = span * rows
    tile = window // ncol
    width = embed_table.shape[1]
    chans = proj_row.shape[1]
    layers = pair_weights.shape[0]
    kernel = conv_first.shape[0] // width
    half = kernel // 2
    edge = 2 * HALO
    total = span + tile + 4 * edge
    height, wide = span + 2 * HALO, tile + 2 * HALO
    n_pair = height // 2
    two = 2 * chans
    vmem = pl.BlockSpec(memory_space=pltpu.VMEM)
    hbm = pl.BlockSpec(memory_space=pltpu.HBM)
    left, right, weights = pl.pallas_call(
        functools.partial(sequence_kernel, (rows, ncol, span, tile, chans, kernel, layers)),
        out_shape=(
            jax.ShapeDtypeStruct((n_pair, two), F32),
            jax.ShapeDtypeStruct((wide, two), F32),
            jax.ShapeDtypeStruct((layers, 4 * chans, 6 * chans), BF16),
        ),
        in_specs=[hbm] * 7,
        out_specs=(vmem, vmem, vmem),
        scratch_shapes=[
            pltpu.VMEM((rows, 1, span), jnp.int32),
            pltpu.VMEM(embed_table.shape, BF16),
            pltpu.VMEM(conv_first.shape, BF16),
            pltpu.VMEM(conv_second.shape, BF16),
            pltpu.VMEM((chans, width), BF16),
            pltpu.VMEM((chans, width), BF16),
            pltpu.VMEM(pair_weights.shape, BF16),
            pltpu.SemaphoreType.DMA((7,)),
            pltpu.SemaphoreType.DMA((rows,)),
            pltpu.SemaphoreType.DMA((rows,)),
            pltpu.VMEM((32, width), BF16),
            pltpu.VMEM((window + 2 * edge, width), F32),
            pltpu.VMEM((total, width), F32),
            pltpu.VMEM((total - 2 * half, width), F32),
            pltpu.VMEM((total - 2 * half, kernel * width), BF16),
            pltpu.VMEM((height, two), F32),
            pltpu.VMEM((height, two), F32),
            pltpu.VMEM((wide, two), F32),
        ],
        compiler_params=pltpu.CompilerParams(
            vmem_limit_bytes=60 * 1024 * 1024, collective_id=0, has_side_effects=True
        ),
        name="sequence",
    )(residues.reshape(1, span), embed_table, conv_first, conv_second, proj_row.T, proj_col.T, pair_weights)
    return pl.pallas_call(
        functools.partial(pair_kernel, (rows, ncol, span, tile, chans, layers)),
        out_shape=jax.ShapeDtypeStruct((chans, span, tile), BF16),
        in_specs=[vmem, vmem, hbm],
        out_specs=hbm,
        scratch_shapes=[
            pltpu.VMEM((layers, 4 * chans, 6 * chans), BF16),
            pltpu.VMEM((n_pair, wide, two), F32),
            pltpu.VMEM((n_pair + 2 * PAD, wide, two), BF16),
            pltpu.VMEM((n_pair + 2 * PAD, wide, two), BF16),
            pltpu.VMEM((4, wide, two), F32),
            pltpu.VMEM((tile // 128, chans * span, 128), F32),
            pltpu.VMEM((chans, span, tile), BF16),
            pltpu.VMEM((3, wide, two), BF16),
            pltpu.SemaphoreType.DMA((1 + CHUNKS,)),
        ],
        compiler_params=pltpu.CompilerParams(vmem_limit_bytes=40000 * 1024),
        name="pairs",
    )(left, right, weights)


def solution(mesh):
    return jax.shard_map(
        local,
        mesh=mesh,
        in_specs=(P("row"), P(), P(), P(), P(), P(), P()),
        out_specs=P(None, "row", "col"),
        check_vma=False,
    )
```

```python
import functools

import jax
import jax.numpy as jnp
from jax import lax
from jax.experimental import pallas as pl
from jax.experimental.pallas import tpu as pltpu
from jax.sharding import PartitionSpec as P

MESH = pl.DeviceIdType.MESH
STRIPS = 16
CHUNKS = 4
STEP = 18
LIMIT = 67043328
TAPS = 4
HALO = 16
F32, BF16 = jnp.float32, jnp.bfloat16


def elu(v):
    return jnp.maximum(v, jnp.exp(jnp.minimum(v, 0.0)) - 1.0)


def sequence_kernel(
    dims, res_hbm, table_hbm, w1_hbm, w2_hbm, prow_hbm, pcol_hbm, pw_hbm, left_out, right_out, bw,
    res_ref, table_ref, w1_ref, w2_ref, prow_ref, pcol_ref, pw_ref, sems, send_sem, recv_sem,
    taps, fs, tmp, right_ref,
):
    rows, ncol, span, tile, chans, kernel, layers = dims
    me_r, me_c = lax.axis_index("row"), lax.axis_index("col")
    window = rows * span
    vocab, width = table_ref.shape
    half = kernel // 2
    edge = 2 * HALO
    n_row, n_col = span + 2 * edge, tile + 2 * edge
    height, wide = span + 2 * HALO, tile + 2 * HALO
    two = 2 * chans

    around, per_col = edge // span, tile // span
    low, high = me_c * per_col - around, (me_c + 1) * per_col + around

    def takes(source, target):
        near = (source - target <= around) & (target - source <= around)
        return near | ((source >= low) & (source < high))

    peers = [lax.rem(me_r + k, rows) for k in range(1, rows)]
    barrier = pltpu.get_barrier_semaphore()
    for peer in peers:

        @pl.when(takes(peer, me_r))
        def _(peer=peer):
            pl.semaphore_signal(barrier, inc=1, device_id={"row": peer}, device_id_type=MESH)

    pairs = (
        (res_hbm, res_ref.at[me_r]), (table_hbm, table_ref), (w1_hbm, w1_ref), (pw_hbm, pw_ref),
        (w2_hbm, w2_ref), (prow_hbm, prow_ref), (pcol_hbm, pcol_ref),
    )
    loads = [pltpu.make_async_copy(a, b, sems.at[i]) for i, (a, b) in enumerate(pairs)]
    for load in loads:
        load.start()

    expected = sum(takes(me_r, peer).astype(jnp.int32) for peer in peers)
    pl.semaphore_wait(barrier, expected)
    copies = [
        pltpu.make_async_remote_copy(
            src_ref=res_hbm,
            dst_ref=res_ref.at[me_r],
            send_sem=send_sem.at[k],
            recv_sem=recv_sem.at[k],
            device_id={"row": peer},
            device_id_type=MESH,
        )
        for k, peer in enumerate(peers)
    ]
    for copy, peer in zip(copies, peers):

        @pl.when(takes(me_r, peer))
        def _(copy=copy):
            copy.start()

    slot = 1 << (vocab - 1).bit_length()
    share = 128 // slot
    groups = -(-kernel // share)
    loads[1].wait()
    loads[2].wait()
    table = jnp.concatenate([table_ref[...], jnp.zeros((slot - vocab, width), BF16)], axis=0)
    for k in range(kernel):
        row = jnp.dot(table, w1_ref[k * width : (k + 1) * width, :], preferred_element_type=F32)
        taps[k * slot : (k + 1) * slot, :] = row.astype(BF16)
    taps[kernel * slot :, :] = jnp.zeros((groups * 128 - kernel * slot, width), BF16)

    loads[3].wait()
    zero = jnp.zeros((chans, chans), BF16)
    for layer in range(layers):
        w = pw_ref[layer].astype(F32).T.astype(BF16)
        for g, offset in enumerate((0, 1, 2, -1)):
            line = []
            for tx in range(3):
                for h in range(2):
                    ty = offset - h + 1
                    tap = 3 * ty + tx
                    here = 0 <= ty <= 2
                    line.append(w[tap * chans : (tap + 1) * chans] if here else zero)
            bw[layer, g * chans : (g + 1) * chans, :] = jnp.concatenate(line, axis=1)
    for load in loads[4:]:
        load.wait()

    loads[0].wait()
    for k, copy in enumerate(copies):
        source = lax.rem(me_r + rows - 1 - k, rows)

        @pl.when(takes(source, me_r))
        def _(copy=copy):
            copy.wait_recv()

        @pl.when(takes(me_r, peers[k]))
        def _(copy=copy):
            copy.wait_send()

    shards = [me_r + i - around for i in range(n_row // span)]
    shards += [low + i for i in range(n_col // span)]
    pieces = []
    for shard in shards:
        piece = res_ref[jnp.clip(shard, 0, rows - 1)]
        pieces.append(jnp.where((shard >= 0) & (shard < rows), piece, -1).astype(F32))
    total = n_row + n_col
    padded = -(-(total + 8) // 128) * 128
    if padded > total:
        pieces.append(jnp.full((1, padded - total), -1.0, F32))
    line = jnp.concatenate(pieces, axis=1)
    one = jnp.ones((128, 128), BF16)
    at = lax.broadcasted_iota(jnp.int32, (128, 128), 0)
    lane = lax.broadcasted_iota(jnp.int32, (128, 128), 1)
    for g in range(padded // 128):
        diagonal = jnp.where(at == lane, line[:, 128 * g : 128 * (g + 1)], 0.0).astype(BF16)
        tmp[128 * g : 128 * (g + 1), :] = jnp.dot(diagonal, one, preferred_element_type=F32)
    n_first = total - 2 * half
    reach = n_first + share * (groups - 1)
    lanes = lax.broadcasted_iota(jnp.int32, (reach, 128), 1)
    seen = tmp[0:reach, :]
    for i in range(1, share):
        seen = jnp.where(lanes < slot * i, seen, tmp[i : i + reach, :])
    fs[0:reach, 0:128] = seen
    kind = lax.rem(lax.broadcasted_iota(jnp.int32, (n_first, 128), 1), slot).astype(F32)
    hot = jnp.concatenate(
        [
            jnp.where(fs[share * g : share * g + n_first, 0:128] == kind, 1.0, 0.0).astype(BF16)
            for g in range(groups)
        ],
        axis=1,
    )
    first = elu(jnp.dot(hot, taps[...], preferred_element_type=F32))
    at = lax.broadcasted_iota(jnp.int32, (n_first, width), 0) + half
    pos = at + jnp.where(at < n_row, me_r * span - edge, me_c * tile - edge - n_row)
    first = jnp.where((pos >= 0) & (pos < window), first, 0.0)
    fs[0:n_first, :] = first.astype(BF16).astype(F32)

    acc = None
    for g in range(0, kernel, TAPS):
        some = range(g, min(g + TAPS, kernel))
        lhs = jnp.concatenate(
            [
                jnp.concatenate(
                    [fs[k : k + height, :], fs[k + n_row : k + n_row + wide, :]], axis=0
                ).astype(BF16)
                for k in some
            ],
            axis=1,
        )
        w2 = w2_ref[g * width : (some[-1] + 1) * width, :]
        got = jnp.dot(lhs, w2, preferred_element_type=F32)
        acc = got if acc is None else acc + got
    centre = jnp.concatenate(
        [fs[half : half + height, :], fs[half + n_row : half + n_row + wide, :]], axis=0
    )
    second = (centre + elu(acc)).astype(BF16)

    def project(x, w):
        both = jnp.concatenate([w, w], axis=0)
        y = lax.dot_general(x, both, (((1,), (1,)), ((), ())), preferred_element_type=F32)
        return y.astype(BF16).astype(F32)

    tmp[0:height, :] = project(second[0:height], prow_ref[...])
    right_ref[...] = project(second[height : height + wide], pcol_ref[...])
    n_pair = height // 2
    half_lane = lax.broadcasted_iota(jnp.int32, (n_pair, two), 1) < chans
    left_out[...] = jnp.where(
        half_lane, tmp[pl.ds(0, n_pair, stride=2), :], tmp[pl.ds(1, n_pair, stride=2), :]
    )
    slabs = wide // STRIPS
    for m in range(slabs):
        right_out[STRIPS * m : STRIPS * (m + 1)] = right_ref[pl.ds(m, STRIPS, stride=slabs), :]


def pair_kernel(
    dims, left_hbm, right_hbm, bw_hbm, out_hbm, left_ref, right_ref, bw, pair, act_a, act_b, lin, stage, outv, masks, sems
):
    rows, ncol, span, tile, chans, layers = dims
    me_r, me_c = lax.axis_index("row"), lax.axis_index("col")
    n_pair = (span + 2 * HALO) // 2
    wide, two = tile + 2 * HALO, 2 * chans
    slabs = wide // STRIPS
    moves = ((left_hbm, left_ref), (right_hbm, right_ref), (bw_hbm, bw))
    loads = [pltpu.make_async_copy(a, b, sems.at[i]) for i, (a, b) in enumerate(moves)]
    for load in loads:
        load.start()

    at = lax.broadcasted_iota(jnp.int32, (wide, two), 0)
    col = lax.rem(at, STRIPS) * slabs + lax.div(at, STRIPS)
    inside = ((col >= HALO) | (me_c > 0)) & ((col < HALO + tile) | (me_c < ncol - 1))
    inside = jnp.where(inside, 1.0, 0.0)
    masks[0] = inside.astype(BF16)
    masks[1] = (inside * (me_r > 0).astype(F32)).astype(BF16)
    masks[2] = (inside * (me_r < rows - 1).astype(F32)).astype(BF16)
    lane = lax.broadcasted_iota(jnp.int32, (wide, two), 1)
    low_bf16 = lane.astype(F32).astype(BF16) < jnp.asarray(chans, BF16)
    low_half = lane < chans

    def put(act, p, value):
        pair[p] = value
        if isinstance(p, int):
            which = 1 if p < HALO // 2 else 2 if p >= n_pair - HALO // 2 else 0
        else:
            which = jnp.where(p < HALO // 2, 1, jnp.where(p >= n_pair - HALO // 2, 2, 0))
        act[p] = elu(value).astype(BF16) * masks[which]

    def start(p):
        put(act_a, p, right_ref[...] + left_ref[pl.ds(p, 1), :])

    def shifted(part, d):
        if d > 0:
            ends = [part[STRIPS * m : STRIPS * (m + 1)] for m in range(slabs - d, slabs)]
            ends = [pltpu.roll(e, 1, 0) for e in ends]
            return jnp.concatenate(ends + [part[: STRIPS * (slabs - d)]], axis=0)
        ends = [part[STRIPS * m : STRIPS * (m + 1)] for m in range(-d)]
        ends = [pltpu.roll(e, STRIPS - 1, 0) for e in ends]
        return jnp.concatenate([part[STRIPS * -d :]] + ends, axis=0)

    def conv(layer, src, d, slots):
        lhs = jnp.concatenate(
            [
                jnp.concatenate(
                    [src[p], jnp.where(low_bf16, src[p + d], src[p - d])], axis=1
                )
                for p in slots
            ],
            axis=0,
        )
        got = jnp.dot(lhs, bw[layer], preferred_element_type=F32)
        values = []
        for k, p in enumerate(slots):
            part = got[k * wide : (k + 1) * wide]
            total = shifted(part[:, 0:two], d) + part[:, two : 2 * two]
            total = total + shifted(part[:, 2 * two : 3 * two], -d)
            values.append(pair[p] + total)
        return values

    loads[0].wait()
    loads[1].wait()
    bufs = (act_a, act_b)
    for layer in range(layers - 1):
        src, dst = bufs[layer % 2], bufs[(layer + 1) % 2]
        d = 2**layer
        if layer == 0:
            def begin(p, _):
                start(p)
                return 0

            lax.fori_loop(0, n_pair, begin, 0, unroll=4)
            loads[2].wait()

        def step(q, _, rim=False, layer=layer, src=src, dst=dst, d=d):
            if rim:
                slots = [q + d, n_pair - 2 * d + q]
            else:
                x = 2 * d * lax.div(q, d) + lax.rem(q, d)
                slots = [x, x + d]
            one, other = conv(layer, src, d, slots)
            if rim:
                new = [pltpu.roll(one, chans, 1), one, other, pltpu.roll(other, chans, 1)]
                slots = [q, q + d, n_pair - 2 * d + q, n_pair - d + q]
            else:
                new = [
                    jnp.where(low_half, one, pltpu.roll(other, chans, 1)),
                    jnp.where(low_half, pltpu.roll(one, chans, 1), other),
                ]
            for p, value in zip(slots, new):
                put(dst, p, value)
            return 0

        n_main = n_pair // 2 - 2 * d
        lax.fori_loop(d, d + n_main, step, 0, unroll=n_main // 2)
        for q in range(d):
            step(q, 0, rim=True)

    src = bufs[(layers - 1) % 2]
    d = 2 ** (layers - 1)
    halves = tile // 128
    for u in range((n_pair - HALO) // 2):
        slots = (HALO // 2 + 2 * u, HALO // 2 + 2 * u + 1)
        for k, value in enumerate(conv(layers - 1, src, d, slots)):
            b = lin.at[(2 * u + k) % 4]
            for m in range(slabs):
                b[pl.ds(m, STRIPS, stride=slabs), :] = value[STRIPS * m : STRIPS * (m + 1)]
            turned = b[HALO : HALO + tile, :].T
            at = slots[k] - HALO // 2
            line = 2 * d * (at // d) + at % d
            for h in range(halves):
                block = turned[:, 128 * h : 128 * (h + 1)]
                for i, rows_of in ((line, block[0:chans]), (line + d, block[chans:two])):
                    stage[h, i // 16, pl.ds(i % 16, chans, stride=STEP), :] = rows_of
    step = chans // CHUNKS
    saves = []
    for g in range(CHUNKS):
        for c in range(g * step, (g + 1) * step):
            for h in range(halves):
                for r in range(span // 16):
                    got = stage[h, r, STEP * c : STEP * c + 16, :]
                    outv[c, 16 * r : 16 * (r + 1), 128 * h : 128 * (h + 1)] = got.astype(BF16)
        part = pl.ds(g * step, step)
        saves.append(pltpu.make_async_copy(outv.at[part], out_hbm.at[part], sems.at[3 + g]))
        saves[-1].start()
    for save in saves:
        save.wait()


def local(residues, embed_table, conv_first, conv_second, proj_row, proj_col, pair_weights):
    rows, ncol = lax.axis_size("row"), lax.axis_size("col")
    span = residues.shape[0]
    window = span * rows
    tile = window // ncol
    width = embed_table.shape[1]
    chans = proj_row.shape[1]
    layers = pair_weights.shape[0]
    kernel = conv_first.shape[0] // width
    edge = 2 * HALO
    slot = 1 << (embed_table.shape[0] - 1).bit_length()
    padded = -(-(span + tile + 4 * edge + 8) // 128) * 128
    height, wide = span + 2 * HALO, tile + 2 * HALO
    n_pair = height // 2
    two = 2 * chans
    vmem = pl.BlockSpec(memory_space=pltpu.VMEM)
    hbm = pl.BlockSpec(memory_space=pltpu.HBM)
    left, right, weights = pl.pallas_call(
        functools.partial(sequence_kernel, (rows, ncol, span, tile, chans, kernel, layers)),
        out_shape=(
            jax.ShapeDtypeStruct((n_pair, two), F32),
            jax.ShapeDtypeStruct((wide, two), F32),
            jax.ShapeDtypeStruct((layers, 4 * chans, 6 * chans), BF16),
        ),
        in_specs=[hbm] * 7,
        out_specs=(vmem, vmem, vmem),
        scratch_shapes=[
            pltpu.VMEM((rows, 1, span), jnp.int32),
            pltpu.VMEM(embed_table.shape, BF16),
            pltpu.VMEM(conv_first.shape, BF16),
            pltpu.VMEM(conv_second.shape, BF16),
            pltpu.VMEM((chans, width), BF16),
            pltpu.VMEM((chans, width), BF16),
            pltpu.VMEM(pair_weights.shape, BF16),
            pltpu.SemaphoreType.DMA((7,)),
            pltpu.SemaphoreType.DMA((rows,)),
            pltpu.SemaphoreType.DMA((rows,)),
            pltpu.VMEM((-(-kernel * slot // 128) * 128, width), BF16),
            pltpu.VMEM((padded, width), F32),
            pltpu.VMEM((padded, two), F32),
            pltpu.VMEM((wide, two), F32),
        ],
        compiler_params=pltpu.CompilerParams(
            vmem_limit_bytes=LIMIT, collective_id=0, has_side_effects=True
        ),
        name="sequence",
    )(residues.reshape(1, span), embed_table, conv_first, conv_second, proj_row.T, proj_col.T, pair_weights)
    return pl.pallas_call(
        functools.partial(pair_kernel, (rows, ncol, span, tile, chans, layers)),
        out_shape=jax.ShapeDtypeStruct((chans, span, tile), BF16),
        in_specs=[hbm] * 3,
        out_specs=hbm,
        scratch_shapes=[
            pltpu.VMEM((n_pair, two), F32),
            pltpu.VMEM((wide, two), F32),
            pltpu.VMEM((layers, 4 * chans, 6 * chans), BF16),
            pltpu.VMEM((n_pair, wide, two), F32),
            pltpu.VMEM((n_pair, wide, two), BF16),
            pltpu.VMEM((n_pair, wide, two), BF16),
            pltpu.VMEM((4, wide, two), F32),
            pltpu.VMEM((tile // 128, span // 16, chans * STEP, 128), F32),
            pltpu.VMEM((chans, span, tile), BF16),
            pltpu.VMEM((3, wide, two), BF16),
            pltpu.SemaphoreType.DMA((3 + CHUNKS,)),
        ],
        compiler_params=pltpu.CompilerParams(vmem_limit_bytes=LIMIT),
        name="pairs",
    )(left, right, weights)


def solution(mesh):
    return jax.shard_map(
        local,
        mesh=mesh,
        in_specs=(P("row"), P(), P(), P(), P(), P(), P()),
        out_specs=P(None, "row", "col"),
        check_vma=False,
    )
```

```python
import functools

import jax
import jax.numpy as jnp
from jax import lax
from jax.experimental import pallas as pl
from jax.experimental.pallas import tpu as pltpu
from jax.sharding import PartitionSpec as P

MESH = pl.DeviceIdType.MESH
STRIPS = 16
STEP = 18
LIMIT = 67043328 - 163840
TAPS = 4
HALO = 16
F32, BF16 = jnp.float32, jnp.bfloat16


def elu(v):
    return jnp.maximum(v, jnp.exp(jnp.minimum(v, 0.0)) - 1.0)


def sequence_kernel(
    dims, res_hbm, table_hbm, w1_hbm, w2_hbm, prow_hbm, pcol_hbm, pw_hbm, left_out, right_out, bw_out,
    res_ref, table_ref, w1_ref, w2_ref, prow_ref, pcol_ref, pw_ref, sems, send_sem, recv_sem, ready,
    taps, fs, tmp, right_ref, bw,
):
    rows, ncol, span, tile, chans, kernel, layers = dims
    me_r, me_c = lax.axis_index("row"), lax.axis_index("col")
    window = rows * span
    vocab, width = table_ref.shape
    half = kernel // 2
    edge = 2 * HALO
    n_row, n_col = span + 2 * edge, tile + 2 * edge
    height, wide = span + 2 * HALO, tile + 2 * HALO
    two = 2 * chans

    around, per_col = edge // span, tile // span
    low, high = me_c * per_col - around, (me_c + 1) * per_col + around

    def takes(source, target):
        near = (source - target <= around) & (target - source <= around)
        return near | ((source >= low) & (source < high))

    def related(r):
        return takes(me_r, r) | takes(r, me_r)

    barrier = pltpu.get_barrier_semaphore()
    for r in range(rows):

        @pl.when((r > me_r) & related(r))
        def _(r=r):
            pl.semaphore_signal(barrier, inc=1, device_id={"row": r}, device_id_type=MESH)

    pairs = (
        (res_hbm, res_ref.at[me_r]), (table_hbm, table_ref), (w1_hbm, w1_ref), (pw_hbm, pw_ref),
        (w2_hbm, w2_ref), (prow_hbm, prow_ref), (pcol_hbm, pcol_ref),
    )
    loads = [pltpu.make_async_copy(a, b, sems.at[i]) for i, (a, b) in enumerate(pairs)]
    for load in loads:
        load.start()

    greeted = sum(((r < me_r) & related(r)).astype(jnp.int32) for r in range(rows))

    @pl.when(me_r > 0)
    def _():
        pl.semaphore_wait(barrier, greeted)

    for r in range(rows):

        @pl.when((r < me_r) & takes(r, me_r))
        def _(r=r):
            pl.semaphore_signal(
                ready.at[me_r], inc=1, device_id={"row": r}, device_id_type=MESH
            )

    copies = [
        pltpu.make_async_remote_copy(
            src_ref=res_hbm,
            dst_ref=res_ref.at[me_r],
            send_sem=send_sem.at[r],
            recv_sem=recv_sem.at[me_r],
            device_id={"row": r},
            device_id_type=MESH,
        )
        for r in range(rows)
    ]
    for r in range(rows):

        @pl.when((r < me_r) & takes(me_r, r))
        def _(r=r):
            copies[r].start()

    slot = 1 << (vocab - 1).bit_length()
    share = 128 // slot
    groups = -(-kernel // share)
    loads[1].wait()
    loads[2].wait()
    table = jnp.concatenate([table_ref[...], jnp.zeros((slot - vocab, width), BF16)], axis=0)
    for k in range(kernel):
        row = jnp.dot(table, w1_ref[k * width : (k + 1) * width, :], preferred_element_type=F32)
        taps[k * slot : (k + 1) * slot, :] = row.astype(BF16)
    taps[kernel * slot :, :] = jnp.zeros((groups * 128 - kernel * slot, width), BF16)

    loads[3].wait()
    zero = jnp.zeros((chans, chans), BF16)
    for layer in range(layers):
        w = pw_ref[layer].astype(F32).T.astype(BF16)
        for g, offset in enumerate((0, 1, 2, -1)):
            line = []
            for tx in range(3):
                for h in range(2):
                    ty = offset - h + 1
                    tap = 3 * ty + tx
                    here = 0 <= ty <= 2
                    line.append(w[tap * chans : (tap + 1) * chans] if here else zero)
            bw[layer, g * chans : (g + 1) * chans, :] = jnp.concatenate(line, axis=1)
    save = pltpu.make_async_copy(bw, bw_out, sems.at[len(pairs)])
    save.start()
    for r in range(rows):

        @pl.when((r > me_r) & takes(me_r, r))
        def _(r=r):
            pl.semaphore_wait(ready.at[r], 1)
            copies[r].start()

    for load in loads[4:]:
        load.wait()
    loads[0].wait()
    for r in range(rows):

        @pl.when((r != me_r) & takes(r, me_r))
        def _(r=r):
            pltpu.make_async_remote_copy(
                src_ref=res_hbm,
                dst_ref=res_ref.at[r],
                send_sem=send_sem.at[r],
                recv_sem=recv_sem.at[r],
                device_id={"row": r},
                device_id_type=MESH,
            ).wait_recv()

        @pl.when((r != me_r) & takes(me_r, r))
        def _(r=r):
            copies[r].wait_send()

    shards = [me_r + i - around for i in range(n_row // span)]
    shards += [low + i for i in range(n_col // span)]
    pieces = []
    for shard in shards:
        piece = res_ref[jnp.clip(shard, 0, rows - 1)]
        pieces.append(jnp.where((shard >= 0) & (shard < rows), piece, -1).astype(F32))
    total = n_row + n_col
    padded = -(-(total + 8) // 128) * 128
    if padded > total:
        pieces.append(jnp.full((1, padded - total), -1.0, F32))
    line = jnp.concatenate(pieces, axis=1)
    one = jnp.ones((128, 128), BF16)
    at = lax.broadcasted_iota(jnp.int32, (128, 128), 0)
    lane = lax.broadcasted_iota(jnp.int32, (128, 128), 1)
    for g in range(padded // 128):
        diagonal = jnp.where(at == lane, line[:, 128 * g : 128 * (g + 1)], 0.0).astype(BF16)
        tmp[128 * g : 128 * (g + 1), :] = jnp.dot(diagonal, one, preferred_element_type=F32)
    n_first = total - 2 * half
    reach = n_first + share * (groups - 1)
    lanes = lax.broadcasted_iota(jnp.int32, (reach, 128), 1)
    seen = tmp[0:reach, :]
    for i in range(1, share):
        seen = jnp.where(lanes < slot * i, seen, tmp[i : i + reach, :])
    fs[0:reach, 0:128] = seen
    kind = lax.rem(lax.broadcasted_iota(jnp.int32, (n_first, 128), 1), slot).astype(F32)
    hot = jnp.concatenate(
        [
            jnp.where(fs[share * g : share * g + n_first, 0:128] == kind, 1.0, 0.0).astype(BF16)
            for g in range(groups)
        ],
        axis=1,
    )
    first = elu(jnp.dot(hot, taps[...], preferred_element_type=F32))
    at = lax.broadcasted_iota(jnp.int32, (n_first, width), 0) + half
    pos = at + jnp.where(at < n_row, me_r * span - edge, me_c * tile - edge - n_row)
    first = jnp.where((pos >= 0) & (pos < window), first, 0.0)
    fs[0:n_first, :] = first.astype(BF16).astype(F32)

    acc = None
    for g in range(0, kernel, TAPS):
        some = range(g, min(g + TAPS, kernel))
        lhs = jnp.concatenate(
            [
                jnp.concatenate(
                    [fs[k : k + height, :], fs[k + n_row : k + n_row + wide, :]], axis=0
                ).astype(BF16)
                for k in some
            ],
            axis=1,
        )
        w2 = w2_ref[g * width : (some[-1] + 1) * width, :]
        got = jnp.dot(lhs, w2, preferred_element_type=F32)
        acc = got if acc is None else acc + got
    centre = jnp.concatenate(
        [fs[half : half + height, :], fs[half + n_row : half + n_row + wide, :]], axis=0
    )
    second = (centre + elu(acc)).astype(BF16)

    def project(x, w):
        both = jnp.concatenate([w, w], axis=0)
        y = lax.dot_general(x, both, (((1,), (1,)), ((), ())), preferred_element_type=F32)
        return y.astype(BF16).astype(F32)

    tmp[0:height, :] = project(second[0:height], prow_ref[...])
    right_ref[...] = project(second[height : height + wide], pcol_ref[...])
    n_pair = height // 2
    half_lane = lax.broadcasted_iota(jnp.int32, (n_pair, two), 1) < chans
    left_out[...] = jnp.where(
        half_lane, tmp[pl.ds(0, n_pair, stride=2), :], tmp[pl.ds(1, n_pair, stride=2), :]
    )
    slabs = wide // STRIPS
    for m in range(slabs):
        right_out[STRIPS * m : STRIPS * (m + 1)] = right_ref[pl.ds(m, STRIPS, stride=slabs), :]
    save.wait()


def pair_kernel(
    dims, left_ref, right_ref, bw_hbm, out_hbm, bw, pair, act_a, act_b, lin, stage, outv, masks, sems
):
    rows, ncol, span, tile, chans, layers = dims
    me_r, me_c = lax.axis_index("row"), lax.axis_index("col")
    n_pair = (span + 2 * HALO) // 2
    wide, two = tile + 2 * HALO, 2 * chans
    slabs = wide // STRIPS
    moves = ((bw_hbm, bw),)
    loads = [pltpu.make_async_copy(a, b, sems.at[i]) for i, (a, b) in enumerate(moves)]
    for load in loads:
        load.start()

    at = lax.broadcasted_iota(jnp.int32, (wide, two), 0)
    col = lax.rem(at, STRIPS) * slabs + lax.div(at, STRIPS)
    inside = ((col >= HALO) | (me_c > 0)) & ((col < HALO + tile) | (me_c < ncol - 1))
    inside = jnp.where(inside, 1.0, 0.0)
    masks[0] = inside.astype(BF16)
    masks[1] = (inside * (me_r > 0).astype(F32)).astype(BF16)
    masks[2] = (inside * (me_r < rows - 1).astype(F32)).astype(BF16)
    lane = lax.broadcasted_iota(jnp.int32, (wide, two), 1)
    low_bf16 = lane.astype(F32).astype(BF16) < jnp.asarray(chans, BF16)
    low_half = lane < chans

    def put(act, p, value):
        pair[p] = value
        if isinstance(p, int):
            which = 1 if p < HALO // 2 else 2 if p >= n_pair - HALO // 2 else 0
        else:
            which = jnp.where(p < HALO // 2, 1, jnp.where(p >= n_pair - HALO // 2, 2, 0))
        act[p] = elu(value).astype(BF16) * masks[which]

    def start(p):
        put(act_a, p, right_ref[...] + left_ref[pl.ds(p, 1), :])

    def shifted(part, d):
        if d > 0:
            ends = [part[STRIPS * m : STRIPS * (m + 1)] for m in range(slabs - d, slabs)]
            ends = [pltpu.roll(e, 1, 0) for e in ends]
            return jnp.concatenate(ends + [part[: STRIPS * (slabs - d)]], axis=0)
        ends = [part[STRIPS * m : STRIPS * (m + 1)] for m in range(-d)]
        ends = [pltpu.roll(e, STRIPS - 1, 0) for e in ends]
        return jnp.concatenate([part[STRIPS * -d :]] + ends, axis=0)

    def conv(layer, src, d, slots):
        lhs = jnp.concatenate(
            [
                jnp.concatenate(
                    [src[p], jnp.where(low_bf16, src[p + d], src[p - d])], axis=1
                )
                for p in slots
            ],
            axis=0,
        )
        got = jnp.dot(lhs, bw[layer], preferred_element_type=F32)
        values = []
        for k, p in enumerate(slots):
            part = got[k * wide : (k + 1) * wide]
            total = shifted(part[:, 0:two], d) + part[:, two : 2 * two]
            total = total + shifted(part[:, 2 * two : 3 * two], -d)
            values.append(pair[p] + total)
        return values

    bufs = (act_a, act_b)
    for layer in range(layers - 1):
        src, dst = bufs[layer % 2], bufs[(layer + 1) % 2]
        d = 2**layer
        if layer == 0:
            def begin(p, _):
                start(p)
                return 0

            lax.fori_loop(0, n_pair, begin, 0, unroll=4)
            loads[0].wait()

        def step(q, _, rim=False, layer=layer, src=src, dst=dst, d=d):
            if rim:
                slots = [q + d, n_pair - 2 * d + q]
            else:
                x = 2 * d * lax.div(q, d) + lax.rem(q, d)
                slots = [x, x + d]
            one, other = conv(layer, src, d, slots)
            if rim:
                new = [pltpu.roll(one, chans, 1), one, other, pltpu.roll(other, chans, 1)]
                slots = [q, q + d, n_pair - 2 * d + q, n_pair - d + q]
            else:
                new = [
                    jnp.where(low_half, one, pltpu.roll(other, chans, 1)),
                    jnp.where(low_half, pltpu.roll(one, chans, 1), other),
                ]
            for p, value in zip(slots, new):
                put(dst, p, value)
            return 0

        n_main = n_pair // 2 - 2 * d
        lax.fori_loop(d, d + n_main, step, 0, unroll=n_main // 2)
        for q in range(d):
            step(q, 0, rim=True)

    src = bufs[(layers - 1) % 2]
    d = 2 ** (layers - 1)
    halves = tile // 128
    saves = []
    for u in range((n_pair - HALO) // 2):
        slots = (HALO // 2 + 2 * u, HALO // 2 + 2 * u + 1)
        for k, value in enumerate(conv(layers - 1, src, d, slots)):
            b = lin.at[(2 * u + k) % 4]
            for m in range(slabs):
                b[pl.ds(m, STRIPS, stride=slabs), :] = value[STRIPS * m : STRIPS * (m + 1)]
            turned = b[HALO : HALO + tile, :].T
            at = slots[k] - HALO // 2
            line = 2 * d * (at // d) + at % d
            for h in range(halves):
                block = turned[:, 128 * h : 128 * (h + 1)]
                for i, rows_of in ((line, block[0:chans]), (line + d, block[chans:two])):
                    stage[h, i // 16, pl.ds(i % 16, chans, stride=STEP), :] = rows_of
        if (2 * u + 2) % d == 0:
            group = 2 * d
            r = (2 * u + 2) // d - 1
            for c in range(chans):
                for h in range(halves):
                    got = stage[h, r, STEP * c : STEP * c + group, :]
                    outv[c, group * r : group * (r + 1), 128 * h : 128 * (h + 1)] = got.astype(BF16)
            part = pl.ds(group * r, group)
            saves.append(pltpu.make_async_copy(outv.at[:, part], out_hbm.at[:, part], sems.at[1 + r]))
            saves[-1].start()
    for save in saves:
        save.wait()


def local(residues, embed_table, conv_first, conv_second, proj_row, proj_col, pair_weights):
    rows, ncol = lax.axis_size("row"), lax.axis_size("col")
    span = residues.shape[0]
    window = span * rows
    tile = window // ncol
    width = embed_table.shape[1]
    chans = proj_row.shape[1]
    layers = pair_weights.shape[0]
    kernel = conv_first.shape[0] // width
    edge = 2 * HALO
    slot = 1 << (embed_table.shape[0] - 1).bit_length()
    padded = -(-(span + tile + 4 * edge + 8) // 128) * 128
    height, wide = span + 2 * HALO, tile + 2 * HALO
    n_pair = height // 2
    two = 2 * chans
    vmem = pl.BlockSpec(memory_space=pltpu.VMEM)
    hbm = pl.BlockSpec(memory_space=pltpu.HBM)
    left, right, weights = pl.pallas_call(
        functools.partial(sequence_kernel, (rows, ncol, span, tile, chans, kernel, layers)),
        out_shape=(
            pltpu.VMEM((n_pair, two), F32),
            pltpu.VMEM((wide, two), F32),
            jax.ShapeDtypeStruct((layers, 4 * chans, 6 * chans), BF16),
        ),
        in_specs=[hbm] * 7,
        out_specs=(vmem, vmem, hbm),
        scratch_shapes=[
            pltpu.VMEM((rows, 1, span), jnp.int32),
            pltpu.VMEM(embed_table.shape, BF16),
            pltpu.VMEM(conv_first.shape, BF16),
            pltpu.VMEM(conv_second.shape, BF16),
            pltpu.VMEM((chans, width), BF16),
            pltpu.VMEM((chans, width), BF16),
            pltpu.VMEM(pair_weights.shape, BF16),
            pltpu.SemaphoreType.DMA((8,)),
            pltpu.SemaphoreType.DMA((rows,)),
            pltpu.SemaphoreType.DMA((rows,)),
            pltpu.SemaphoreType.REGULAR((rows,)),
            pltpu.VMEM((-(-kernel * slot // 128) * 128, width), BF16),
            pltpu.VMEM((padded, width), F32),
            pltpu.VMEM((padded, two), F32),
            pltpu.VMEM((wide, two), F32),
            pltpu.VMEM((layers, 4 * chans, 6 * chans), BF16),
        ],
        compiler_params=pltpu.CompilerParams(
            vmem_limit_bytes=LIMIT, collective_id=0, has_side_effects=True
        ),
        name="sequence",
    )(residues.reshape(1, span), embed_table, conv_first, conv_second, proj_row.T, proj_col.T, pair_weights)
    left = pltpu.with_memory_space_constraint(left, pltpu.VMEM)
    right = pltpu.with_memory_space_constraint(right, pltpu.VMEM)
    return pl.pallas_call(
        functools.partial(pair_kernel, (rows, ncol, span, tile, chans, layers)),
        out_shape=jax.ShapeDtypeStruct((chans, span, tile), BF16),
        in_specs=[vmem, vmem, hbm],
        out_specs=hbm,
        scratch_shapes=[
            pltpu.VMEM((layers, 4 * chans, 6 * chans), BF16),
            pltpu.VMEM((n_pair, wide, two), F32),
            pltpu.VMEM((n_pair, wide, two), BF16),
            pltpu.VMEM((n_pair, wide, two), BF16),
            pltpu.VMEM((4, wide, two), F32),
            pltpu.VMEM((tile // 128, span // 16, chans * STEP, 128), F32),
            pltpu.VMEM((chans, span, tile), BF16),
            pltpu.VMEM((3, wide, two), BF16),
            pltpu.SemaphoreType.DMA((1 + span // 16,)),
        ],
        compiler_params=pltpu.CompilerParams(vmem_limit_bytes=LIMIT - 409600),
        name="pairs",
    )(left, right, weights)


def solution(mesh):
    return jax.shard_map(
        local,
        mesh=mesh,
        in_specs=(P("row"), P(), P(), P(), P(), P(), P()),
        out_specs=P(None, "row", "col"),
        check_vma=False,
    )
```

```python
import functools

import jax
import jax.numpy as jnp
from jax import lax
from jax.experimental import pallas as pl
from jax.experimental.pallas import tpu as pltpu
from jax.sharding import PartitionSpec as P

MESH = pl.DeviceIdType.MESH
STRIPS = 16
GROUP = 4
STEP = 18
LIMIT = 67043328 - 163840
TAPS = 4
HALO = 16
F32, BF16 = jnp.float32, jnp.bfloat16


def elu(v):
    return jnp.maximum(v, jnp.exp(jnp.minimum(v, 0.0)) - 1.0)


def turned_over(layer, block, t):
    return block % 2 if layer % 2 == 0 else int(t >= 2 ** (layer - 1))


def swaps(layer, f):
    return 1 - f if layer % 2 == 0 else f


def sequence_kernel(
    dims, res_hbm, table_hbm, w1_hbm, w2_hbm, prow_hbm, pcol_hbm, pw_hbm, left_out, right_out, bw_out,
    res_ref, table_ref, w1_ref, w2_ref, prow_ref, pcol_ref, pw_ref, sems, send_sem, recv_sem, ready,
    taps, fs, tmp, right_ref, bw,
):
    rows, ncol, span, tile, chans, kernel, layers = dims
    me_r, me_c = lax.axis_index("row"), lax.axis_index("col")
    window = rows * span
    vocab, width = table_ref.shape
    half = kernel // 2
    edge = 2 * HALO
    n_row, n_col = span + 2 * edge, tile + 2 * edge
    height, wide = span + 2 * HALO, tile + 2 * HALO
    two = 2 * chans

    around, per_col = edge // span, tile // span
    low, high = me_c * per_col - around, (me_c + 1) * per_col + around

    def takes(source, target):
        near = (source - target <= around) & (target - source <= around)
        return near | ((source >= low) & (source < high))

    def related(r):
        return takes(me_r, r) | takes(r, me_r)

    barrier = pltpu.get_barrier_semaphore()
    for r in range(rows):

        @pl.when((r > me_r) & related(r))
        def _(r=r):
            pl.semaphore_signal(barrier, inc=1, device_id={"row": r}, device_id_type=MESH)

    pairs = (
        (res_hbm, res_ref.at[me_r]), (table_hbm, table_ref), (w1_hbm, w1_ref), (pw_hbm, pw_ref),
        (w2_hbm, w2_ref), (prow_hbm, prow_ref), (pcol_hbm, pcol_ref),
    )
    loads = [pltpu.make_async_copy(a, b, sems.at[i]) for i, (a, b) in enumerate(pairs)]
    for load in loads:
        load.start()

    greeted = sum(((r < me_r) & related(r)).astype(jnp.int32) for r in range(rows))

    @pl.when(me_r > 0)
    def _():
        pl.semaphore_wait(barrier, greeted)

    for r in range(rows):

        @pl.when((r < me_r) & takes(r, me_r))
        def _(r=r):
            pl.semaphore_signal(
                ready.at[me_r], inc=1, device_id={"row": r}, device_id_type=MESH
            )

    copies = [
        pltpu.make_async_remote_copy(
            src_ref=res_hbm,
            dst_ref=res_ref.at[me_r],
            send_sem=send_sem.at[r],
            recv_sem=recv_sem.at[me_r],
            device_id={"row": r},
            device_id_type=MESH,
        )
        for r in range(rows)
    ]
    for r in range(rows):

        @pl.when((r < me_r) & takes(me_r, r))
        def _(r=r):
            copies[r].start()

    slot = 1 << (vocab - 1).bit_length()
    share = 128 // slot
    groups = -(-kernel // share)
    loads[1].wait()
    loads[2].wait()
    table = jnp.concatenate([table_ref[...], jnp.zeros((slot - vocab, width), BF16)], axis=0)
    for k in range(kernel):
        row = jnp.dot(table, w1_ref[k * width : (k + 1) * width, :], preferred_element_type=F32)
        taps[k * slot : (k + 1) * slot, :] = row.astype(BF16)
    taps[kernel * slot :, :] = jnp.zeros((groups * 128 - kernel * slot, width), BF16)

    loads[3].wait()
    zero = jnp.zeros((chans, chans), BF16)
    for layer in range(layers):
        w = pw_ref[layer].astype(F32).T.astype(BF16)
        for f in range(2):
            beside = (2, -1) if swaps(layer, f) == 0 else (-1, 2)
            for g, offset in enumerate(((0, 1) if f == 0 else (1, 0)) + beside):
                line = []
                for tx in range(3):
                    for h in (0, 1) if f == 0 else (1, 0):
                        ty = offset - h + 1
                        tap = 3 * ty + tx
                        here = 0 <= ty <= 2
                        line.append(w[tap * chans : (tap + 1) * chans] if here else zero)
                bw[layer, f, g * chans : (g + 1) * chans, :] = jnp.concatenate(line, axis=1)
    save = pltpu.make_async_copy(bw, bw_out, sems.at[len(pairs)])
    save.start()
    for r in range(rows):

        @pl.when((r > me_r) & takes(me_r, r))
        def _(r=r):
            pl.semaphore_wait(ready.at[r], 1)
            copies[r].start()

    for load in loads[4:]:
        load.wait()
    loads[0].wait()
    for r in range(rows):

        @pl.when((r != me_r) & takes(r, me_r))
        def _(r=r):
            pltpu.make_async_remote_copy(
                src_ref=res_hbm,
                dst_ref=res_ref.at[r],
                send_sem=send_sem.at[r],
                recv_sem=recv_sem.at[r],
                device_id={"row": r},
                device_id_type=MESH,
            ).wait_recv()

        @pl.when((r != me_r) & takes(me_r, r))
        def _(r=r):
            copies[r].wait_send()

    shards = [me_r + i - around for i in range(n_row // span)]
    shards += [low + i for i in range(n_col // span)]
    pieces = []
    for shard in shards:
        piece = res_ref[jnp.clip(shard, 0, rows - 1)]
        pieces.append(jnp.where((shard >= 0) & (shard < rows), piece, -1).astype(F32))
    total = n_row + n_col
    padded = -(-(total + 8) // 128) * 128
    if padded > total:
        pieces.append(jnp.full((1, padded - total), -1.0, F32))
    line = jnp.concatenate(pieces, axis=1)
    one = jnp.ones((128, 128), BF16)
    at = lax.broadcasted_iota(jnp.int32, (128, 128), 0)
    lane = lax.broadcasted_iota(jnp.int32, (128, 128), 1)
    for g in range(padded // 128):
        diagonal = jnp.where(at == lane, line[:, 128 * g : 128 * (g + 1)], 0.0).astype(BF16)
        tmp[128 * g : 128 * (g + 1), :] = jnp.dot(diagonal, one, preferred_element_type=F32)
    n_first = total - 2 * half
    reach = n_first + share * (groups - 1)
    lanes = lax.broadcasted_iota(jnp.int32, (reach, 128), 1)
    seen = tmp[0:reach, :]
    for i in range(1, share):
        seen = jnp.where(lanes < slot * i, seen, tmp[i : i + reach, :])
    fs[0:reach, 0:128] = seen
    kind = lax.rem(lax.broadcasted_iota(jnp.int32, (n_first, 128), 1), slot).astype(F32)
    hot = jnp.concatenate(
        [
            jnp.where(fs[share * g : share * g + n_first, 0:128] == kind, 1.0, 0.0).astype(BF16)
            for g in range(groups)
        ],
        axis=1,
    )
    first = elu(jnp.dot(hot, taps[...], preferred_element_type=F32))
    at = lax.broadcasted_iota(jnp.int32, (n_first, width), 0) + half
    pos = at + jnp.where(at < n_row, me_r * span - edge, me_c * tile - edge - n_row)
    first = jnp.where((pos >= 0) & (pos < window), first, 0.0)
    fs[0:n_first, :] = first.astype(BF16).astype(F32)

    acc = None
    for g in range(0, kernel, TAPS):
        some = range(g, min(g + TAPS, kernel))
        lhs = jnp.concatenate(
            [
                jnp.concatenate(
                    [fs[k : k + height, :], fs[k + n_row : k + n_row + wide, :]], axis=0
                ).astype(BF16)
                for k in some
            ],
            axis=1,
        )
        w2 = w2_ref[g * width : (some[-1] + 1) * width, :]
        got = jnp.dot(lhs, w2, preferred_element_type=F32)
        acc = got if acc is None else acc + got
    centre = jnp.concatenate(
        [fs[half : half + height, :], fs[half + n_row : half + n_row + wide, :]], axis=0
    )
    second = (centre + elu(acc)).astype(BF16)

    def project(x, w):
        both = jnp.concatenate([w, w], axis=0)
        y = lax.dot_general(x, both, (((1,), (1,)), ((), ())), preferred_element_type=F32)
        return y.astype(BF16).astype(F32)

    tmp[0:height, :] = project(second[0:height], prow_ref[...])
    right_ref[...] = project(second[height : height + wide], pcol_ref[...])
    n_pair = height // 2
    half_lane = lax.broadcasted_iota(jnp.int32, (n_pair, two), 1) < chans
    odd = lax.rem(lax.broadcasted_iota(jnp.int32, (n_pair, two), 0), 2) == 1
    half_lane = half_lane != odd
    left_out[...] = jnp.where(
        half_lane, tmp[pl.ds(0, n_pair, stride=2), :], tmp[pl.ds(1, n_pair, stride=2), :]
    )
    slabs = wide // STRIPS
    for m in range(slabs):
        right_out[STRIPS * m : STRIPS * (m + 1)] = right_ref[pl.ds(m, STRIPS, stride=slabs), :]
    save.wait()


def pair_kernel(
    dims, left_ref, right_ref, bw_hbm, out_hbm, bw, pair, act_a, act_b, lin, stage, outv, masks, sems
):
    rows, ncol, span, tile, chans, layers = dims
    me_r, me_c = lax.axis_index("row"), lax.axis_index("col")
    n_pair = (span + 2 * HALO) // 2
    wide, two = tile + 2 * HALO, 2 * chans
    slabs = wide // STRIPS
    moves = ((bw_hbm, bw),)
    loads = [pltpu.make_async_copy(a, b, sems.at[i]) for i, (a, b) in enumerate(moves)]
    for load in loads:
        load.start()

    at = lax.broadcasted_iota(jnp.int32, (wide, two), 0)
    col = lax.rem(at, STRIPS) * slabs + lax.div(at, STRIPS)
    inside = ((col >= HALO) | (me_c > 0)) & ((col < HALO + tile) | (me_c < ncol - 1))
    inside = jnp.where(inside, 1.0, 0.0)
    masks[0] = inside.astype(BF16)
    masks[1] = (inside * (me_r > 0).astype(F32)).astype(BF16)
    masks[2] = (inside * (me_r < rows - 1).astype(F32)).astype(BF16)
    lane = lax.broadcasted_iota(jnp.int32, (wide, two), 1)
    lane = lane[0:STRIPS]
    low_bf16 = lane.astype(F32).astype(BF16) < jnp.asarray(chans, BF16)
    low_half = lane < chans

    def put(act, p, value):
        pair[p] = value
        which = jnp.where(p < HALO // 2, 1, jnp.where(p >= n_pair - HALO // 2, 2, 0))
        act[p] = elu(value).astype(BF16) * masks[which]

    def start(p):
        put(act_a, p, right_ref[...] + left_ref[pl.ds(p, 1), :])

    def slab(m):
        return pl.ds(STRIPS * m, STRIPS)

    def put_slab(act, p, m, value):
        pair[p, slab(m), :] = value
        which = 1 if p < HALO // 2 else 2 if p >= n_pair - HALO // 2 else 0
        act[p, slab(m), :] = elu(value).astype(BF16) * masks[which, slab(m), :]

    def chain(d):
        return [m for t in range(min(d, slabs)) for m in range(t, slabs, d)]

    def conv(layer, src, d, slots, f):
        order = chain(d)
        place = {m: i for i, m in enumerate(order)}
        after, before = (d, -d) if swaps(layer, f) == 0 else (-d, d)
        lhs = jnp.concatenate(
            [
                jnp.concatenate(
                    [
                        src[p, slab(m), :],
                        jnp.where(low_bf16, src[p + after, slab(m), :], src[p + before, slab(m), :]),
                    ],
                    axis=1,
                )
                for p in slots
                for m in order
            ],
            axis=0,
        )
        got = jnp.dot(lhs, bw[layer, f], preferred_element_type=F32)

        def piece(k, m, tx):
            at = k * wide + STRIPS * place[m % slabs]
            part = got[at : at + STRIPS, tx * two : (tx + 1) * two]
            if m < 0:
                return pltpu.roll(part, 1, 0)
            return part if m < slabs else pltpu.roll(part, STRIPS - 1, 0)

        def value(p, m):
            k = slots.index(p)
            total = piece(k, m - d, 0) + piece(k, m, 1) + piece(k, m + d, 2)
            return pair[p, slab(m), :] + total

        return {p: value for p in slots}

    def convs(layer, src, d, slots):
        values = {}
        for f in range(2):
            some = [p for p in slots if turned_over(layer, p // d, p % d) == f]
            if some:
                values.update(conv(layer, src, d, some, f))
        return values

    bufs = (act_a, act_b)
    for layer in range(layers - 1):
        src, dst = bufs[layer % 2], bufs[(layer + 1) % 2]
        d = 2**layer
        if layer == 0:
            def begin(p, _):
                start(p)
                return 0

            lax.fori_loop(0, n_pair, begin, 0, unroll=4)
            loads[0].wait()

        def place(layer, d, r, x):
            low_here = (r % 2) == turned_over(layer, x // d + r // 2, x % d)
            target = x + (r % 2) * d
            over = turned_over(layer + 1, target // (2 * d), target % (2 * d))
            return target, (r // 2) == over, low_here

        units = [(q + d,) for q in range(d)] + [(n_pair - 2 * d + q,) for q in range(d)]
        for q in range(d, n_pair // 2 - d):
            x = 2 * d * (q // d) + q % d
            units.append((x, x + d))
        for i, unit in enumerate(units):
            if i % GROUP == 0:
                some = units[i : i + GROUP]
                values = convs(layer, src, d, [p for each in some for p in each])
            x = 2 * d * (unit[0] // (2 * d)) + unit[0] % d
            rows_in = [2 * ((p - x) // d) + j for p in unit for j in range(2)]
            for m in chain(d):
                got = {p: values[p](p, m) for p in unit}
                moved = {}
                new = {}
                for r in rows_in:
                    p = x + (r // 2) * d
                    target, low_there, low_here = place(layer, d, r, x)
                    if low_there == low_here:
                        v = got[p]
                    else:
                        if p not in moved:
                            moved[p] = pltpu.roll(got[p], chans, 1)
                        v = moved[p]
                    new.setdefault(target, {})[low_there] = v
                for target, sides in new.items():
                    if len(sides) == 2:
                        v = jnp.where(low_half, sides[True], sides[False])
                    else:
                        v = next(iter(sides.values()))
                    put_slab(dst, target, m, v)

    src = bufs[(layers - 1) % 2]
    d = 2 ** (layers - 1)
    halves = tile // 128
    saves = []
    everyone = list(range(HALO // 2, n_pair - HALO // 2))
    values = convs(layers - 1, src, d, everyone)
    for u in range((n_pair - HALO) // 2):
        slots = (HALO // 2 + 2 * u, HALO // 2 + 2 * u + 1)
        for k, p in enumerate(slots):
            b = lin.at[(2 * u + k) % 4]
            for m in chain(d):
                b[pl.ds(m, STRIPS, stride=slabs), :] = values[p](p, m)
            turned = b[HALO : HALO + tile, :].T
            at = p - HALO // 2
            line = 2 * d * (at // d) + at % d
            for h in range(halves):
                block = turned[:, 128 * h : 128 * (h + 1)]
                over = turned_over(layers - 1, p // d, p % d)
                ends = (line + d, line) if over else (line, line + d)
                for i, rows_of in ((ends[0], block[0:chans]), (ends[1], block[chans:two])):
                    stage[h, i // 16, pl.ds(i % 16, chans, stride=STEP), :] = rows_of
        if (2 * u + 2) % d == 0:
            group = 2 * d
            r = (2 * u + 2) // d - 1
            for c in range(chans):
                for h in range(halves):
                    got = stage[h, r, STEP * c : STEP * c + group, :]
                    outv[c, group * r : group * (r + 1), 128 * h : 128 * (h + 1)] = got.astype(BF16)
            part = pl.ds(group * r, group)
            saves.append(pltpu.make_async_copy(outv.at[:, part], out_hbm.at[:, part], sems.at[1 + r]))
            saves[-1].start()
    for save in saves:
        save.wait()


def local(residues, embed_table, conv_first, conv_second, proj_row, proj_col, pair_weights):
    rows, ncol = lax.axis_size("row"), lax.axis_size("col")
    span = residues.shape[0]
    window = span * rows
    tile = window // ncol
    width = embed_table.shape[1]
    chans = proj_row.shape[1]
    layers = pair_weights.shape[0]
    kernel = conv_first.shape[0] // width
    edge = 2 * HALO
    slot = 1 << (embed_table.shape[0] - 1).bit_length()
    padded = -(-(span + tile + 4 * edge + 8) // 128) * 128
    height, wide = span + 2 * HALO, tile + 2 * HALO
    n_pair = height // 2
    two = 2 * chans
    vmem = pl.BlockSpec(memory_space=pltpu.VMEM)
    hbm = pl.BlockSpec(memory_space=pltpu.HBM)
    left, right, weights = pl.pallas_call(
        functools.partial(sequence_kernel, (rows, ncol, span, tile, chans, kernel, layers)),
        out_shape=(
            pltpu.VMEM((n_pair, two), F32),
            pltpu.VMEM((wide, two), F32),
            jax.ShapeDtypeStruct((layers, 2, 4 * chans, 6 * chans), BF16),
        ),
        in_specs=[hbm] * 7,
        out_specs=(vmem, vmem, hbm),
        scratch_shapes=[
            pltpu.VMEM((rows, 1, span), jnp.int32),
            pltpu.VMEM(embed_table.shape, BF16),
            pltpu.VMEM(conv_first.shape, BF16),
            pltpu.VMEM(conv_second.shape, BF16),
            pltpu.VMEM((chans, width), BF16),
            pltpu.VMEM((chans, width), BF16),
            pltpu.VMEM(pair_weights.shape, BF16),
            pltpu.SemaphoreType.DMA((8,)),
            pltpu.SemaphoreType.DMA((rows,)),
            pltpu.SemaphoreType.DMA((rows,)),
            pltpu.SemaphoreType.REGULAR((rows,)),
            pltpu.VMEM((-(-kernel * slot // 128) * 128, width), BF16),
            pltpu.VMEM((padded, width), F32),
            pltpu.VMEM((padded, two), F32),
            pltpu.VMEM((wide, two), F32),
            pltpu.VMEM((layers, 2, 4 * chans, 6 * chans), BF16),
        ],
        compiler_params=pltpu.CompilerParams(
            vmem_limit_bytes=LIMIT, collective_id=0, has_side_effects=True
        ),
        name="sequence",
    )(residues.reshape(1, span), embed_table, conv_first, conv_second, proj_row.T, proj_col.T, pair_weights)
    left = pltpu.with_memory_space_constraint(left, pltpu.VMEM)
    right = pltpu.with_memory_space_constraint(right, pltpu.VMEM)
    return pl.pallas_call(
        functools.partial(pair_kernel, (rows, ncol, span, tile, chans, layers)),
        out_shape=jax.ShapeDtypeStruct((chans, span, tile), BF16),
        in_specs=[vmem, vmem, hbm],
        out_specs=hbm,
        scratch_shapes=[
            pltpu.VMEM((layers, 2, 4 * chans, 6 * chans), BF16),
            pltpu.VMEM((n_pair, wide, two), F32),
            pltpu.VMEM((n_pair, wide, two), BF16),
            pltpu.VMEM((n_pair, wide, two), BF16),
            pltpu.VMEM((4, wide, two), F32),
            pltpu.VMEM((tile // 128, span // 16, chans * STEP, 128), F32),
            pltpu.VMEM((chans, span, tile), BF16),
            pltpu.VMEM((3, wide, two), BF16),
            pltpu.SemaphoreType.DMA((1 + span // 16,)),
        ],
        compiler_params=pltpu.CompilerParams(vmem_limit_bytes=LIMIT - 409600),
        name="pairs",
    )(left, right, weights)


def solution(mesh):
    return jax.shard_map(
        local,
        mesh=mesh,
        in_specs=(P("row"), P(), P(), P(), P(), P(), P()),
        out_specs=P(None, "row", "col"),
        check_vma=False,
    )
```
